32 devices in a mesh: section: 4 (over y, x), vocab: 8 (over z, core), dp: 1.
Axes of the slice: x: 2, y: 2, z: 4, core: 2. Of those that a mesh axis runs over, the one named last changes fastest.
Arguments:
- hidden: bfloat16 [1, 512, 3072], P('dp', ('section', 'vocab')), may hold values from -160 to 160
- head: bfloat16 [131072, 3072], P(('section', 'vocab')), may hold values from -3 to 3
- labels: int32 [1, 512], P('dp'), may hold values from 0 to 131071
- response_mask: int32 [1, 512], P('dp'), may hold values from 0 to 1, as said below
- seq_pair: int32 [1, 4], P('dp'), may hold values from 0 to 3, as said below
- ref_logp: float32 [4], replicated, may hold values from -12.6 to -12.4
Outputs:
- token_logprob: float32 [1, 512], P('dp', ('section', 'vocab'))
- pair_margin: float32 [2], replicated
- loss: float32 [], replicated
The draws below stay inside these ranges and needn't reach their ends.
Inputs may be any that keep to these rules, and one draw needn't show every extreme that they name: `response_mask`: each sequence of 128 rows has more than half of its rows set. `seq_pair`: over all replicas every slot of 0 to 3 appears once; slot q belongs to pair q // 2 and is its chosen response when q is even.
All inputs are finite; a program needn't handle non-finite values.
Results may differ from the reference program's by a relative error of at most 0.0003.
Values may be sent and summed in bfloat16 or wider, within the bound.
A program may use at most 64 MiB of HBM per device.

```python
import jax
import jax.numpy as jnp
from jax import lax

D = 3072
VOCAB = 131072
SEQ_DP = 4
REPLICAS = 1
GROUP_ROWS = 512
SEQS = 4


def head_scale(indices):
    return 0.4 + 2.0 * indices.astype(jnp.float32) / VOCAB


def head_row(key, index):
    stream = jax.random.fold_in(jax.random.fold_in(key, 101), index)
    values = jnp.clip(jax.random.normal(stream, (D,), jnp.float32), -4.0, 4.0)
    return values * head_scale(index) * D ** (-0.5)


def draw_head(key, part):
    indices = jnp.arange(VOCAB, dtype=jnp.int32)
    table = jax.vmap(lambda index: head_row(key, index))(indices)
    return table.astype(jnp.bfloat16)


def draw_hidden(key, part):
    count_rows = REPLICAS * GROUP_ROWS
    values = jnp.clip(jax.random.normal(jax.random.fold_in(key, 201), (count_rows, D), jnp.float32), -6.0, 6.0)
    return values.reshape(REPLICAS, GROUP_ROWS, D).astype(jnp.bfloat16)


def draw_response_mask(key, part):
    seq_len = GROUP_ROWS // SEQ_DP
    prompt = jax.random.randint(jax.random.fold_in(key, 301), (REPLICAS, SEQ_DP, 1), seq_len // 8, seq_len // 2)
    places = jnp.arange(seq_len, dtype=jnp.int32)[None, None, :]
    return (places >= prompt).astype(jnp.int32).reshape(REPLICAS, GROUP_ROWS)


def draw_seq_pair(key, part):
    order = jax.random.permutation(jax.random.fold_in(key, 401), REPLICAS * SEQ_DP)
    return order.astype(jnp.int32).reshape(REPLICAS, SEQ_DP)


def plant(result, own_key, low, top_value):
    shape = result.shape
    place = [jax.random.randint(jax.random.fold_in(own_key, axis), (), 0, shape[axis]) for axis in range(len(shape))]
    result = result.at[tuple(place)].set(low)
    longest = shape.index(max(shape))
    place[longest] = (place[longest] + 1) % shape[longest]
    return result.at[tuple(place)].set(top_value)


def setup_inputs(seed: int = 0) -> dict:
    splits = jax.random.split(jax.random.key(seed), 7)
    return {
        "hidden": draw_hidden(jax.random.fold_in(splits[6], 71), 0),
        "head": draw_head(jax.random.fold_in(splits[6], 71), 0),
        "labels": plant(jax.random.randint(splits[2], (REPLICAS, GROUP_ROWS), 0, VOCAB), jax.random.fold_in(splits[2], 1), 0, VOCAB - 1).astype(jnp.int32),
        "response_mask": draw_response_mask(jax.random.fold_in(splits[6], 71), 0),
        "seq_pair": draw_seq_pair(jax.random.fold_in(splits[6], 71), 0),
        "ref_logp": jnp.clip(jax.random.uniform(splits[5], (SEQS,), jnp.float32, -12.6, -12.4), -12.6, -12.4),
    }


beta_scale = 5.0


def reference(hidden, head, labels, response_mask, seq_pair, ref_logp):
    def replica_logp(packed):
        states, targets = packed
        logits = lax.dot_general(states, head, (((1,), (1,)), ((), ())), preferred_element_type=jnp.float32)
        top_logit = jnp.max(logits, axis=1)
        total = jnp.sum(jnp.exp(logits - top_logit[:, None]), axis=1)
        target_logit = jnp.take_along_axis(logits, targets[:, None], axis=1)[:, 0]
        return target_logit - top_logit - jnp.log(total)

    token_logprob = lax.map(replica_logp, (hidden, labels))
    weights = response_mask.astype(jnp.float32)
    seq_len = GROUP_ROWS // SEQ_DP
    sums = jnp.sum((token_logprob * weights).reshape(REPLICAS, SEQ_DP, seq_len), axis=2)
    counts = jnp.sum(weights.reshape(REPLICAS, SEQ_DP, seq_len), axis=2)
    means = (sums / counts).reshape(SEQS)
    slot_ids = jnp.arange(SEQS, dtype=jnp.int32)
    in_pair = (seq_pair.reshape(SEQS)[:, None] == slot_ids[None, :]).astype(jnp.float32)
    policy = jnp.sum(in_pair * means[:, None], axis=0)
    pair_margin = beta_scale * ((policy[0::2] - ref_logp[0::2]) - (policy[1::2] - ref_logp[1::2]))
    loss = jnp.mean(jnp.logaddexp(0.0, -pair_margin))
    return token_logprob, pair_margin, loss
```

```python
import functools

import jax
import jax.numpy as jnp
from jax import lax
from jax.experimental import pallas as pl
from jax.experimental.pallas import tpu as pltpu
from jax.sharding import PartitionSpec as P

SEQ_DP = 4
CORES = 2
LANES = 128
CHUNKS = 4
TILE = 512
SEGMENTS = 4
LOWEST = -3.0e38

beta_scale = 5.0
MESH = pl.DeviceIdType.MESH


def kernel(
    sections,
    vocab,
    solo,
    hidden_ref,
    head_ref,
    labels_ref,
    mask_ref,
    pair_ref,
    ref_ref,
    token_ref,
    policy_ref,
    margin_ref,
    loss_ref,
    hid,
    headv,
    acc,
    run_max,
    run_sum,
    run_label,
    target_ref,
    stat_a,
    stat_b,
    lp_ref,
    send_sem,
    recv_sem,
    own_sem,
    head_sem,
    stat_send,
    recv_a,
    recv_b,
):
    rows = hidden_ref.shape[1]
    vocab_rows, width = head_ref.shape
    chunk = width // CHUNKS
    all_rows = hid.shape[1]
    floors = vocab // CORES
    s = lax.axis_index("section")
    v = lax.axis_index("vocab")
    z, c = v // CORES, v % CORES
    position = s * vocab + v
    near_a = s + 1 - 2 * (s % 2)
    near_b = (s + 2) % 4
    n1 = (1 - c) * near_a + c * near_b
    n2 = c * near_a + (1 - c) * near_b
    far = 3 - s

    def head_copy(k):
        return pltpu.make_async_copy(
            head_ref.at[:, pl.ds(k * chunk, chunk)], headv.at[k], head_sem.at[k]
        )

    def own_copy(k):
        return pltpu.make_async_copy(
            hidden_ref.at[0, :, pl.ds(k * chunk, chunk)],
            hid.at[k, pl.ds(position * rows, rows)],
            own_sem.at[k],
        )

    def move(k, owner, to_s, to_v, own=False):
        here = hid.at[k, pl.ds(owner * rows, rows)]
        src = hidden_ref.at[0, :, pl.ds(k * chunk, chunk)] if own else here
        return pltpu.make_async_remote_copy(
            src_ref=src,
            dst_ref=here,
            send_sem=send_sem.at[k],
            recv_sem=recv_sem.at[k, owner],
            device_id={"section": to_s, "vocab": to_v},
            device_id_type=MESH,
        )

    other = z * CORES + 1 - c

    def arrived(k, owner):
        move(k, owner, s, other).wait_recv()

    def floor(dz):
        return ((z + dz) % floors) * CORES

    def stage0(k):
        own_copy(k).start()
        for dz in range(1, floors):
            move(k, position, s, floor(dz) + c, True).start()
        move(k, position, n1, v, True).start()
        move(k, position, n2, v, True).start()
        move(k, position, s, other, True).start()

    def stage1(k):
        for dz in range(1, floors):
            owner = s * vocab + floor(dz) + c
            arrived(k, owner)
            move(k, owner, n1, v).start()
            move(k, owner, n2, v).start()
            move(k, owner, s, other).start()

    def stage2(k):
        for dz in range(floors):
            owner = n1 * vocab + floor(dz) + c
            arrived(k, owner)
            move(k, owner, n2, v).start()
            move(k, owner, s, other).start()

    def stage3(k):
        for source in (n2, far):
            for dz in range(floors):
                owner = source * vocab + floor(dz) + c
                arrived(k, owner)
                move(k, owner, s, other).start()

    def stage4(k):
        own_copy(k).wait()
        for section in range(sections):
            for level in range(floors):
                arrived(k, section * vocab + level * CORES + 1 - c)

    stages = (stage0, stage1, stage2, stage3, stage4)

    def run(plan):
        for index, k in plan:
            if k < CHUNKS:
                stages[index](k)

    for k in range(CHUNKS):
        head_copy(k).start()

    barrier = pltpu.get_barrier_semaphore()
    peers = [((s + d) % sections, v) for d in range(1, sections)]
    peers += [(s, (v + d) % vocab) for d in range(1, vocab)]
    for to_s, to_v in peers:
        pl.semaphore_signal(
            barrier, inc=1, device_id={"section": to_s, "vocab": to_v}, device_id_type=MESH
        )
    run_max[...] = jnp.full(run_max.shape, LOWEST, jnp.float32)
    run_sum[...] = jnp.zeros(run_sum.shape, jnp.float32)
    run_label[...] = jnp.zeros(run_label.shape, jnp.float32)
    target_ref[...] = (
        labels_ref[...] - position * vocab_rows - lax.broadcasted_iota(jnp.int32, (8, all_rows), 0)
    )
    pl.semaphore_wait(barrier, len(peers))

    run(((0, 0), (1, 0), (0, 1), (2, 0), (1, 1), (3, 0), (0, 2), (2, 1), (4, 0)))

    def product(k, i):
        return lax.dot_general(
            headv[k, pl.ds(i * TILE, TILE), :],
            hid[k],
            (((1,), (1,)), ((), ())),
            preferred_element_type=jnp.float32,
        )

    def soften(i):
        x = acc[pl.ds(i * TILE, TILE), :].reshape(TILE // 8, 8, all_rows)
        old = run_max[...]
        new = jnp.maximum(old, jnp.max(x, axis=0))
        run_max[...] = new
        run_sum[...] = run_sum[...] * jnp.exp(old - new) + jnp.sum(jnp.exp(x - new[None]), axis=0)
        place = 8 * lax.broadcasted_iota(jnp.int32, x.shape, 0) + i * TILE
        run_label[...] += jnp.sum(jnp.where(place == target_ref[...][None], x, 0.0), axis=0)

    tiles = vocab_rows // TILE
    for k in range(CHUNKS):
        head_copy(k).wait()
        plans = (((3, k + 1), (0, k + 3)), ((1, k + 2),), ((2, k + 2),), ())
        for part in range(SEGMENTS):
            run(plans[part])
            first = part * tiles // SEGMENTS
            last = (part + 1) * tiles // SEGMENTS

            def step(i, carry, k=k):
                here = pl.ds(i * TILE, TILE)
                if k == CHUNKS - 1:

                    @pl.when(i > 0)
                    def _():
                        soften(i - 1)

                if k == 0:
                    acc[here, :] = product(k, i)
                else:
                    acc[here, :] += product(k, i)
                return carry

            if k == CHUNKS - 1:
                if part == 0:

                    def whole(i, carry):
                        here = pl.ds(i * TILE, TILE)
                        soften(i - 1)
                        acc[here, :] += product(CHUNKS - 1, i)
                        return carry

                    acc[pl.ds(0, TILE), :] += product(k, 0)
                    lax.fori_loop(1, tiles, whole, 0)
            else:
                lax.fori_loop(first, last, step, 0)
        run(((4, k + 1),))
    soften(tiles - 1)

    top = jnp.max(run_max[...], axis=0, keepdims=True)
    total = jnp.sum(run_sum[...] * jnp.exp(run_max[...] - top), axis=0, keepdims=True)
    spread = top + jnp.log(total)
    label = jnp.sum(run_label[...], axis=0, keepdims=True)
    lines = all_rows // LANES
    for j in range(lines):
        stat_a[s, pl.ds(j, 1), :] = spread[:, j * LANES : (j + 1) * LANES]
        stat_a[s, pl.ds(lines + j, 1), :] = label[:, j * LANES : (j + 1) * LANES]

    def merge(buffer, count):
        values = [buffer[d] for d in range(count)]
        high = functools.reduce(jnp.maximum, [x[:lines] for x in values])
        weight = sum(jnp.exp(x[:lines] - high) for x in values)
        return high + jnp.log(weight), sum(x[lines:] for x in values)

    def share(buffer, mine, index, recv, to_s, to_v, slot):
        return pltpu.make_async_remote_copy(
            src_ref=buffer.at[mine],
            dst_ref=buffer.at[slot],
            send_sem=stat_send.at[index],
            recv_sem=recv.at[slot],
            device_id={"section": to_s, "vocab": to_v},
            device_id_type=MESH,
        )

    sent = []
    for d in range(1, sections):
        copy = share(stat_a, s, d - 1, recv_a, (s + d) % sections, v, s)
        copy.start()
        sent.append(copy)
    for d in range(1, sections):
        share(stat_a, s, d - 1, recv_a, (s + d) % sections, v, (s + d) % sections).wait_recv()
    spread, label = merge(stat_a, sections)
    stat_b[v, pl.ds(0, lines), :] = spread
    stat_b[v, pl.ds(lines, lines), :] = label
    for d in range(1, vocab):
        copy = share(stat_b, v, sections + d - 2, recv_b, s, (v + d) % vocab, v)
        copy.start()
        sent.append(copy)
    for d in range(1, vocab):
        share(stat_b, v, sections + d - 2, recv_b, s, (v + d) % vocab, (v + d) % vocab).wait_recv()
    spread, label = merge(stat_b, vocab)
    logprob = label - spread
    lp_ref[...] = logprob

    per_line = LANES // rows
    own = lp_ref[pl.ds(position // per_line, 1), :]
    own = pltpu.roll(own, (LANES - (position % per_line) * rows) % LANES, 1)
    token_ref[...] = own[:, :rows]

    per_seq = lines // SEQ_DP
    lane = lax.broadcasted_iota(jnp.int32, (1, LANES), 1)
    policy = jnp.zeros((1, LANES), jnp.float32)
    for q in range(SEQ_DP):
        sums = jnp.zeros((1, LANES), jnp.float32)
        counts = jnp.zeros((1, LANES), jnp.float32)
        for j in range(q * per_seq, (q + 1) * per_seq):
            weight = mask_ref[:, j * LANES : (j + 1) * LANES].astype(jnp.float32)
            sums += logprob[j : j + 1] * weight
            counts += weight
        mean = jnp.sum(sums, axis=1, keepdims=True) / jnp.sum(counts, axis=1, keepdims=True)
        policy += jnp.where(lane == pair_ref[0, q], mean, 0.0)
    policy_ref[...] = policy
    margin = jnp.zeros((1, LANES), jnp.float32)
    loss = jnp.zeros((1, LANES), jnp.float32)
    if solo:
        slots = ref_ref.shape[0]
        refs = jnp.zeros((1, LANES), jnp.float32)
        for q in range(slots):
            refs = jnp.where(lane == q, ref_ref[q], refs)
        gain = policy - refs
        for p in range(slots // 2):
            chosen = jnp.sum(jnp.where(lane == 2 * p, gain, 0.0), axis=1, keepdims=True)
            rejected = jnp.sum(jnp.where(lane == 2 * p + 1, gain, 0.0), axis=1, keepdims=True)
            margin = jnp.where(lane == p, beta_scale * (chosen - rejected), margin)
        soft = jnp.maximum(-margin, 0.0) + jnp.log1p(jnp.exp(-jnp.abs(margin)))
        soft = jnp.where(lane < slots // 2, soft, 0.0)
        loss = jnp.broadcast_to(jnp.sum(soft, axis=1, keepdims=True) / (slots // 2), (1, LANES))
    margin_ref[...] = margin
    loss_ref[...] = loss

    for copy in sent:
        copy.wait_send()
    for k in range(CHUNKS):
        span = hid.at[k, pl.ds(0, all_rows - rows)]
        pltpu.make_async_copy(span, span, send_sem.at[k]).wait()


def body(sections, vocab, replicas, hidden, head, labels, response_mask, seq_pair, ref_logp):
    rows, width = hidden.shape[1:]
    vocab_rows = head.shape[0]
    count = sections * vocab
    all_rows = rows * count
    lines = all_rows // LANES
    f32 = jnp.float32
    vmem = pl.BlockSpec(memory_space=pltpu.VMEM)
    smem = pl.BlockSpec(memory_space=pltpu.SMEM)
    anywhere = pl.BlockSpec(memory_space=pl.ANY)
    solo = replicas == 1
    token, policy, margin, loss = pl.pallas_call(
        functools.partial(kernel, sections, vocab, solo),
        out_shape=(
            jax.ShapeDtypeStruct((1, rows), f32),
            jax.ShapeDtypeStruct((1, LANES), f32),
            jax.ShapeDtypeStruct((1, LANES), f32),
            jax.ShapeDtypeStruct((1, LANES), f32),
        ),
        in_specs=[anywhere, anywhere, vmem, vmem, smem, smem],
        out_specs=(vmem, vmem, vmem, vmem),
        scratch_shapes=[
            pltpu.VMEM((CHUNKS, all_rows, width // CHUNKS), jnp.bfloat16),
            pltpu.VMEM((CHUNKS, vocab_rows, width // CHUNKS), jnp.bfloat16),
            pltpu.VMEM((vocab_rows, all_rows), f32),
            pltpu.VMEM((8, all_rows), f32),
            pltpu.VMEM((8, all_rows), f32),
            pltpu.VMEM((8, all_rows), f32),
            pltpu.VMEM((8, all_rows), jnp.int32),
            pltpu.VMEM((sections, 2 * lines, LANES), f32),
            pltpu.VMEM((vocab, 2 * lines, LANES), f32),
            pltpu.VMEM((lines, LANES), f32),
            pltpu.SemaphoreType.DMA((CHUNKS,)),
            pltpu.SemaphoreType.DMA((CHUNKS, count)),
            pltpu.SemaphoreType.DMA((CHUNKS,)),
            pltpu.SemaphoreType.DMA((CHUNKS,)),
            pltpu.SemaphoreType.DMA((sections + vocab,)),
            pltpu.SemaphoreType.DMA((sections,)),
            pltpu.SemaphoreType.DMA((vocab,)),
        ],
        compiler_params=pltpu.CompilerParams(
            collective_id=0, has_side_effects=True, vmem_limit_bytes=60 * 1024 * 1024
        ),
    )(hidden, head, labels, response_mask, seq_pair, ref_logp)
    slots = ref_logp.shape[0]
    if solo:
        return token, margin[0, : slots // 2], loss[0, 0]
    policy = lax.psum(policy[0, :slots], "dp")
    pair_margin = beta_scale * (policy[0::2] - ref_logp[0::2] - (policy[1::2] - ref_logp[1::2]))
    return token, pair_margin, jnp.mean(jnp.logaddexp(0.0, -pair_margin))


def solution(mesh):
    placed = (
        P("dp", ("section", "vocab"), None),
        P(("section", "vocab"), None),
        P("dp", None),
        P("dp", None),
        P("dp", None),
        P(),
    )
    shape = mesh.shape
    return jax.shard_map(
        functools.partial(body, shape["section"], shape["vocab"], shape["dp"]),
        mesh=mesh,
        in_specs=placed,
        out_specs=(P("dp", ("section", "vocab")), P(), P()),
        check_vma=False,
    )
```

```python
import functools

import jax
import jax.numpy as jnp
from jax import lax
from jax.experimental import pallas as pl
from jax.experimental.pallas import tpu as pltpu
from jax.sharding import PartitionSpec as P

SEQ_DP = 4
CORES = 2
LANES = 128
CHUNKS = 2
TILE = 1024
SEGMENTS = 4
LOWEST = -3.0e38

beta_scale = 5.0
MESH = pl.DeviceIdType.MESH


def kernel(
    sections,
    vocab,
    solo,
    hidden_ref,
    head_ref,
    labels_ref,
    mask_ref,
    pair_ref,
    ref_ref,
    out_ref,
    hid,
    headv,
    acc,
    run_max,
    run_sum,
    run_label,
    target_ref,
    stat_a,
    stat_b,
    lp_ref,
    send_sem,
    recv_sem,
    own_sem,
    head_sem,
    stat_send,
    recv_a,
    recv_b,
):
    rows = hidden_ref.shape[1]
    vocab_rows, width = head_ref.shape
    chunk = width // CHUNKS
    all_rows = hid.shape[1]
    floors = vocab // CORES
    s = lax.axis_index("section")
    v = lax.axis_index("vocab")
    z, c = v // CORES, v % CORES
    position = s * vocab + v
    near_a = s + 1 - 2 * (s % 2)
    near_b = (s + 2) % 4
    n1 = (1 - c) * near_a + c * near_b
    n2 = c * near_a + (1 - c) * near_b
    far = 3 - s

    def head_copy(k):
        return pltpu.make_async_copy(
            head_ref.at[:, pl.ds(k * chunk, chunk)], headv.at[k], head_sem.at[k]
        )

    def own_copy(k):
        return pltpu.make_async_copy(
            hidden_ref.at[0, :, pl.ds(k * chunk, chunk)],
            hid.at[k, pl.ds(position * rows, rows)],
            own_sem.at[k],
        )

    def move(k, owner, to_s, to_v):
        here = hid.at[k, pl.ds(owner * rows, rows)]
        return pltpu.make_async_remote_copy(
            src_ref=here,
            dst_ref=here,
            send_sem=send_sem.at[k],
            recv_sem=recv_sem.at[k, owner],
            device_id={"section": to_s, "vocab": to_v},
            device_id_type=MESH,
        )

    other = z * CORES + 1 - c

    def arrived(k, owner):
        move(k, owner, s, other).wait_recv()

    def floor(dz):
        return ((z + dz) % floors) * CORES

    def stage0(k):
        for dz in range(1, floors):
            move(k, position, s, floor(dz) + c).start()
        move(k, position, n1, v).start()
        move(k, position, n2, v).start()
        move(k, position, s, other).start()

    def stage1(k):
        for dz in range(1, floors):
            owner = s * vocab + floor(dz) + c
            arrived(k, owner)
            move(k, owner, n1, v).start()
            move(k, owner, n2, v).start()
            move(k, owner, s, other).start()

    def stage2(k):
        for dz in range(floors):
            owner = n1 * vocab + floor(dz) + c
            arrived(k, owner)
            move(k, owner, n2, v).start()
            move(k, owner, s, other).start()

    def stage3(k):
        for source in (n2, far):
            for dz in range(floors):
                owner = source * vocab + floor(dz) + c
                arrived(k, owner)
                move(k, owner, s, other).start()

    def stage4(k):
        for section in range(sections):
            for level in range(floors):
                arrived(k, section * vocab + level * CORES + 1 - c)

    stages = (stage0, stage1, stage2, stage3, stage4)

    def run(plan):
        for index, k in plan:
            if k < CHUNKS:
                stages[index](k)

    for k in range(CHUNKS):
        own_copy(k).start()

    barrier = pltpu.get_barrier_semaphore()
    peers = [((s + d) % sections, v) for d in range(1, sections)]
    peers += [(s, (v + d) % vocab) for d in range(1, vocab)]
    for to_s, to_v in peers:
        pl.semaphore_signal(
            barrier, inc=1, device_id={"section": to_s, "vocab": to_v}, device_id_type=MESH
        )
    run_max[...] = jnp.full(run_max.shape, LOWEST, jnp.float32)
    run_sum[...] = jnp.zeros(run_sum.shape, jnp.float32)
    run_label[...] = jnp.zeros(run_label.shape, jnp.float32)
    target_ref[...] = (
        labels_ref[...] - position * vocab_rows - lax.broadcasted_iota(jnp.int32, (8, all_rows), 0)
    )
    for k in range(CHUNKS):
        own_copy(k).wait()
    for k in range(CHUNKS):
        head_copy(k).start()
    pl.semaphore_wait(barrier, len(peers))

    run(((0, 0), (1, 0), (0, 1), (2, 0), (1, 1), (3, 0), (4, 0)))

    def product(k, i):
        return lax.dot_general(
            headv[k, pl.ds(i * TILE, TILE), :],
            hid[k],
            (((1,), (1,)), ((), ())),
            preferred_element_type=jnp.float32,
        )

    def soften(i):
        x = acc[pl.ds(i * TILE, TILE), :].reshape(TILE // 8, 8, all_rows)
        old = run_max[...]
        new = jnp.maximum(old, jnp.max(x, axis=0))
        run_max[...] = new
        run_sum[...] = run_sum[...] * jnp.exp(old - new) + jnp.sum(jnp.exp(x - new[None]), axis=0)
        place = 8 * lax.broadcasted_iota(jnp.int32, x.shape, 0) + i * TILE
        run_label[...] += jnp.sum(jnp.where(place == target_ref[...][None], x, 0.0), axis=0)

    tiles = vocab_rows // TILE
    for k in range(CHUNKS):
        head_copy(k).wait()
        plans = (((2, k + 1), (0, k + 2)), ((1, k + 2),), ((3, k + 1),), ())
        for part in range(SEGMENTS):
            run(plans[part])
            first = part * tiles // SEGMENTS
            last = (part + 1) * tiles // SEGMENTS

            def step(i, carry, k=k):
                here = pl.ds(i * TILE, TILE)
                if k == CHUNKS - 1:

                    @pl.when(i > 0)
                    def _():
                        soften(i - 1)

                if k == 0:
                    acc[here, :] = product(k, i)
                else:
                    acc[here, :] += product(k, i)
                return carry

            if k == CHUNKS - 1:
                if part == 0:

                    def whole(i, carry):
                        here = pl.ds(i * TILE, TILE)
                        soften(i - 1)
                        acc[here, :] += product(CHUNKS - 1, i)
                        return carry

                    acc[pl.ds(0, TILE), :] += product(k, 0)
                    lax.fori_loop(1, tiles, whole, 0)
            else:
                lax.fori_loop(first, last, step, 0)
        run(((4, k + 1),))
    soften(tiles - 1)

    top = jnp.max(run_max[...], axis=0, keepdims=True)
    total = jnp.sum(run_sum[...] * jnp.exp(run_max[...] - top), axis=0, keepdims=True)
    spread = top + jnp.log(total)
    label = jnp.sum(run_label[...], axis=0, keepdims=True)
    lines = all_rows // LANES
    for j in range(lines):
        stat_a[s, pl.ds(j, 1), :] = spread[:, j * LANES : (j + 1) * LANES]
        stat_a[s, pl.ds(lines + j, 1), :] = label[:, j * LANES : (j + 1) * LANES]

    def merge(buffer, count):
        values = [buffer[d] for d in range(count)]
        high = functools.reduce(jnp.maximum, [x[:lines] for x in values])
        weight = sum(jnp.exp(x[:lines] - high) for x in values)
        return high + jnp.log(weight), sum(x[lines:] for x in values)

    def share(buffer, mine, index, recv, to_s, to_v, slot):
        return pltpu.make_async_remote_copy(
            src_ref=buffer.at[mine],
            dst_ref=buffer.at[slot],
            send_sem=stat_send.at[index],
            recv_sem=recv.at[slot],
            device_id={"section": to_s, "vocab": to_v},
            device_id_type=MESH,
        )

    sent = []
    for d in range(1, sections):
        copy = share(stat_a, s, d - 1, recv_a, (s + d) % sections, v, s)
        copy.start()
        sent.append(copy)
    for d in range(1, sections):
        share(stat_a, s, d - 1, recv_a, (s + d) % sections, v, (s + d) % sections).wait_recv()
    spread, label = merge(stat_a, sections)
    stat_b[v, pl.ds(0, lines), :] = spread
    stat_b[v, pl.ds(lines, lines), :] = label
    for d in range(1, vocab):
        copy = share(stat_b, v, sections + d - 2, recv_b, s, (v + d) % vocab, v)
        copy.start()
        sent.append(copy)
    for d in range(1, vocab):
        share(stat_b, v, sections + d - 2, recv_b, s, (v + d) % vocab, (v + d) % vocab).wait_recv()
    spread, label = merge(stat_b, vocab)
    logprob = label - spread
    lp_ref[...] = logprob

    per_line = LANES // rows
    own = lp_ref[pl.ds(position // per_line, 1), :]
    own = pltpu.roll(own, (LANES - (position % per_line) * rows) % LANES, 1)
    out_ref[...] = jnp.zeros(out_ref.shape, jnp.float32)
    out_ref[0:1, :] = own

    per_seq = lines // SEQ_DP
    lane = lax.broadcasted_iota(jnp.int32, (1, LANES), 1)
    policy = jnp.zeros((1, LANES), jnp.float32)
    for q in range(SEQ_DP):
        sums = jnp.zeros((1, LANES), jnp.float32)
        counts = jnp.zeros((1, LANES), jnp.float32)
        for j in range(q * per_seq, (q + 1) * per_seq):
            weight = mask_ref[:, j * LANES : (j + 1) * LANES].astype(jnp.float32)
            sums += logprob[j : j + 1] * weight
            counts += weight
        mean = jnp.sum(sums, axis=1, keepdims=True) / jnp.sum(counts, axis=1, keepdims=True)
        policy += jnp.where(lane == pair_ref[0, q], mean, 0.0)
    margin = jnp.zeros((1, LANES), jnp.float32)
    loss = jnp.zeros((1, LANES), jnp.float32)
    if solo:
        slots = ref_ref.shape[0]
        refs = jnp.zeros((1, LANES), jnp.float32)
        for q in range(slots):
            refs = jnp.where(lane == q, ref_ref[q], refs)
        gain = policy - refs
        for p in range(slots // 2):
            chosen = jnp.sum(jnp.where(lane == 2 * p, gain, 0.0), axis=1, keepdims=True)
            rejected = jnp.sum(jnp.where(lane == 2 * p + 1, gain, 0.0), axis=1, keepdims=True)
            margin = jnp.where(lane == p, beta_scale * (chosen - rejected), margin)
        soft = jnp.maximum(-margin, 0.0) + jnp.log1p(jnp.exp(-jnp.abs(margin)))
        soft = jnp.where(lane < slots // 2, soft, 0.0)
        loss = jnp.broadcast_to(jnp.sum(soft, axis=1, keepdims=True) / (slots // 2), (1, LANES))
    out_ref[1:2, :] = margin
    out_ref[2:3, :] = loss
    out_ref[3:4, :] = policy

    for copy in sent:
        copy.wait_send()
    for k in range(CHUNKS):
        span = hid.at[k, pl.ds(0, all_rows - rows)]
        pltpu.make_async_copy(span, span, send_sem.at[k]).wait()


def body(sections, vocab, replicas, hidden, head, labels, response_mask, seq_pair, ref_logp):
    rows, width = hidden.shape[1:]
    vocab_rows = head.shape[0]
    count = sections * vocab
    all_rows = rows * count
    lines = all_rows // LANES
    f32 = jnp.float32
    vmem = pl.BlockSpec(memory_space=pltpu.VMEM)
    smem = pl.BlockSpec(memory_space=pltpu.SMEM)
    anywhere = pl.BlockSpec(memory_space=pl.ANY)
    solo = replicas == 1
    packed = pl.pallas_call(
        functools.partial(kernel, sections, vocab, solo),
        out_shape=jax.ShapeDtypeStruct((8, LANES), f32),
        in_specs=[anywhere, anywhere, vmem, vmem, smem, smem],
        out_specs=vmem,
        scratch_shapes=[
            pltpu.VMEM((CHUNKS, all_rows, width // CHUNKS), jnp.bfloat16),
            pltpu.VMEM((CHUNKS, vocab_rows, width // CHUNKS), jnp.bfloat16),
            pltpu.VMEM((vocab_rows, all_rows), f32),
            pltpu.VMEM((8, all_rows), f32),
            pltpu.VMEM((8, all_rows), f32),
            pltpu.VMEM((8, all_rows), f32),
            pltpu.VMEM((8, all_rows), jnp.int32),
            pltpu.VMEM((sections, 2 * lines, LANES), f32),
            pltpu.VMEM((vocab, 2 * lines, LANES), f32),
            pltpu.VMEM((lines, LANES), f32),
            pltpu.SemaphoreType.DMA((CHUNKS,)),
            pltpu.SemaphoreType.DMA((CHUNKS, count)),
            pltpu.SemaphoreType.DMA((CHUNKS,)),
            pltpu.SemaphoreType.DMA((CHUNKS,)),
            pltpu.SemaphoreType.DMA((sections + vocab,)),
            pltpu.SemaphoreType.DMA((sections,)),
            pltpu.SemaphoreType.DMA((vocab,)),
        ],
        compiler_params=pltpu.CompilerParams(
            collective_id=0, has_side_effects=True, vmem_limit_bytes=60 * 1024 * 1024
        ),
    )(hidden, head, labels, response_mask, seq_pair, ref_logp)
    slots = ref_logp.shape[0]
    token = packed[:1, :rows]
    if solo:
        return token, packed[1, : slots // 2], packed[2, 0]
    policy = lax.psum(packed[3, :slots], "dp")
    pair_margin = beta_scale * (policy[0::2] - ref_logp[0::2] - (policy[1::2] - ref_logp[1::2]))
    return token, pair_margin, jnp.mean(jnp.logaddexp(0.0, -pair_margin))


def solution(mesh):
    placed = (
        P("dp", ("section", "vocab"), None),
        P(("section", "vocab"), None),
        P("dp", None),
        P("dp", None),
        P("dp", None),
        P(),
    )
    shape = mesh.shape
    return jax.shard_map(
        functools.partial(body, shape["section"], shape["vocab"], shape["dp"]),
        mesh=mesh,
        in_specs=placed,
        out_specs=(P("dp", ("section", "vocab")), P(), P()),
        check_vma=False,
    )
```
